1024 devices in a mesh: seq: 64 (over z, core), head: 16 (over y, x).
Axes of the slice: x: 4, y: 4, z: 32, core: 2. Of those that a mesh axis runs over, the one named last changes fastest.
Arguments:
- queries: bfloat16 [8192, 4096], P(('seq', 'head')), as said below
- keys: bfloat16 [8192, 4096], P('seq', 'head'), as said below
- values: bfloat16 [8192, 4096], P('seq', 'head'), may hold values from -6 to 6
- block_order: int32 [64], replicated, may hold values from 0 to 63, each once
Outputs:
- attended: bfloat16 [8192, 4096], P('seq', 'head')
The draws below stay inside these ranges and needn't reach their ends.
Inputs may be any that keep to these rules, and one draw needn't show every extreme that they name: `block_order`: each storage block holds a different sequence block. `queries`: entries lie within -8 to 8. `keys`: entries lie within -8 to 8.
All inputs are finite; a program needn't handle non-finite values.
Results may differ from the reference program's by a relative error of at most 0.006.
Values may be sent and summed in bfloat16 or wider, within the bound.
A program may use at most 32 MiB of HBM per device.

```python
import jax
import jax.numpy as jnp
from jax import lax

HEADS = 32
HEAD_DIM = 128
TOK_DEV = 128
SEQ_BLOCKS = 64
TOKENS = 8192


def shared_pair(key):
    tokens = TOK_DEV * SEQ_BLOCKS
    width = HEADS * HEAD_DIM
    key_a, key_b = jax.random.split(key, 2)
    q_all = jnp.clip(jax.random.normal(key_a, (tokens, width), jnp.float32), -6.0, 6.0)
    k_all = jnp.clip(jax.random.normal(key_b, (tokens, width), jnp.float32), -6.0, 6.0)
    return (q_all, k_all)


def draw_queries(key, part):
    q_all, k_all = shared_pair(jax.random.fold_in(key, 7))
    return q_all.astype(jnp.bfloat16)


def draw_keys(key, part):
    q_all, k_all = shared_pair(jax.random.fold_in(key, 7))
    return k_all.astype(jnp.bfloat16)


def shard_levels(rng, dims, shards, smallest, top_value):
    def one(axis_at, blocks):
        heights = jax.random.uniform(jax.random.fold_in(jax.random.fold_in(rng, 6), axis_at), (blocks,), jnp.float32, smallest / len(shards), top_value / len(shards))
        return jnp.repeat(jnp.exp(heights), dims[axis_at] // blocks).reshape((-1,) + (1,) * (len(dims) - axis_at - 1))

    loudness = one(*shards[0])
    for cut in shards[1:]:
        loudness = loudness * one(*cut)
    return loudness


def normal_values(stream_key, extent, scale, reach, shards=(), kind=jnp.bfloat16):
    values = jax.random.normal(stream_key, extent, jnp.float32) * scale
    if len(shards) > 0:
        values = shard_levels(stream_key, extent, shards, -0.22, 0.18) * values
    return jnp.clip(values, min=-reach, max=reach).astype(kind)


def setup_inputs(seed: int = 0) -> dict:
    arg_keys = jax.random.split(jax.random.key(seed), 5)
    return {
        "queries": draw_queries(jax.random.fold_in(arg_keys[4], 71), 0),
        "keys": draw_keys(jax.random.fold_in(arg_keys[4], 71), 0),
        "values": normal_values(arg_keys[2], (TOKENS, HEADS * HEAD_DIM), 1.0, 6.0, ((0, 64), (1, 16))),
        "block_order": jax.random.permutation(arg_keys[3], SEQ_BLOCKS).astype(jnp.int32),
    }


def reference(queries, keys, values, block_order):
    tokens = queries.shape[0]
    rows = jnp.arange(tokens, dtype=jnp.int32)
    positions = (block_order[rows // TOK_DEV] * TOK_DEV + rows % TOK_DEV).astype(jnp.int32)
    scale = 1.0 / (HEAD_DIM ** 0.5)
    q_heads = jnp.transpose(queries.reshape(tokens, HEADS, HEAD_DIM), (1, 0, 2))
    k_heads = jnp.transpose(keys.reshape(tokens, HEADS, HEAD_DIM), (1, 0, 2))
    v_heads = jnp.transpose(values.reshape(tokens, HEADS, HEAD_DIM), (1, 0, 2))
    block = 512 if tokens % 512 == 0 else tokens
    q_pos = positions.reshape(tokens // block, block)

    def one_head(operands):
        q_one, k_one, v_one = operands
        q_blocks = q_one.reshape(tokens // block, block, HEAD_DIM)

        def one_block(pieces):
            q_block, pos_block = pieces
            scores = jnp.dot(q_block, k_one.T, preferred_element_type=jnp.float32) * scale
            allowed = positions[None, :] <= pos_block[:, None]
            scores = jnp.where(allowed, scores, jnp.float32(-1e30))
            rowmax = jnp.max(scores, axis=1, keepdims=True)
            weight = jnp.where(allowed, jnp.exp(scores - rowmax), jnp.float32(0.0))
            total = jnp.sum(weight, axis=1, keepdims=True)
            mixed = jnp.dot(weight.astype(jnp.bfloat16), v_one, preferred_element_type=jnp.float32)
            return mixed / total

        out = lax.map(one_block, (q_blocks, q_pos))
        return out.reshape(tokens, HEAD_DIM)

    result = lax.map(one_head, (q_heads, k_heads, v_heads))
    return jnp.transpose(result, (1, 0, 2)).reshape(tokens, HEADS * HEAD_DIM).astype(jnp.bfloat16)
```

```python
import functools
import math

import jax
import jax.numpy as jnp
from jax import lax
from jax.experimental import pallas as pl
from jax.experimental.pallas import tpu as pltpu
from jax.sharding import PartitionSpec as P

D = 128
MESH = pl.DeviceIdType.MESH
NEG = -1e30
SPLIT = 2
COMPUTE = True


def kernel(
    nz, ny, nx,
    order_ref, q_ref, k_ref, v_ref, out_ref,
    buf, qx, qy, qf, qt, m_ref, l_ref, acc_ref, ost, osend,
    ring_sem, sent_sem, part_sem, own_sem, qx_sem, qy_sem, qf_sem, q_sent, o_sem,
):
    seq = lax.axis_index("seq")
    head = lax.axis_index("head")
    z, c = seq // 2, seq % 2
    y, x = head // nx, head % nx
    half = nz // 2
    rows = D // SPLIT
    other = 1 - c

    up = (2 * ((z + 1) % nz) + c, head)
    down = (2 * ((z + nz - 1) % nz) + c, head)
    toward = (up, down)
    partner = (2 * z + other, head)
    along_x = [(seq, y * nx + (x + i) % nx) for i in range(1, nx)]
    along_y = [(seq, ((y + i) % ny) * nx + x) for i in range(1, ny)]

    barrier = pltpu.get_barrier_semaphore()
    peers = [up, down, partner] + along_x + along_y
    for peer in peers:
        pl.semaphore_signal(barrier, inc=1, device_id=peer, device_id_type=MESH)
    pl.semaphore_wait(barrier, len(peers))

    def slot(d, t, kv, j):
        return ((d * (half + 1) + t) * 2 + kv) * 2 + j

    def piece_sem(d, t, kv, j, r):
        return slot(d, t, kv, j) * SPLIT + r

    def cols(which):
        return pl.ds(pl.multiple_of(which * D, D), D)

    def send(src, d, t, kv, j, r):
        pltpu.make_async_remote_copy(
            src_ref=src,
            dst_ref=buf.at[slot(d, t, kv, j), pl.ds(r * rows, rows)],
            send_sem=sent_sem.at[d],
            recv_sem=ring_sem.at[piece_sem(d, t, kv, j, r)],
            device_id=toward[d],
            device_id_type=MESH,
        ).start()

    def arrived(d, t, kv, j, r):
        ref = buf.at[slot(d, t, kv, j), pl.ds(r * rows, rows)]
        pltpu.make_async_copy(ref, ref, ring_sem.at[piece_sem(d, t, kv, j, r)]).wait()

    for kv, ref in enumerate((k_ref, v_ref)):
        for r in range(SPLIT):
            for d in range(2):
                send(ref.at[pl.ds(r * rows, rows), cols(c)], d, 1, kv, c, r)
        pltpu.make_async_remote_copy(
            src_ref=ref.at[:, cols(other)],
            dst_ref=buf.at[slot(0, 0, kv, c)],
            send_sem=own_sem.at[0],
            recv_sem=part_sem.at[kv],
            device_id=partner,
            device_id_type=MESH,
        ).start()
        pltpu.make_async_copy(
            ref.at[:, cols(c)], buf.at[slot(0, 0, kv, c)], own_sem.at[1]
        ).start()

    for i, peer in enumerate(along_x):
        to_x = (x + i + 1) % nx
        for b in range(ny):
            pltpu.make_async_remote_copy(
                src_ref=q_ref.at[:, pl.ds(pl.multiple_of((b * nx + to_x) * 2 * D, D), 2 * D)],
                dst_ref=qx.at[b, x],
                send_sem=q_sent.at[0],
                recv_sem=qx_sem.at[i],
                device_id=peer,
                device_id_type=MESH,
            ).start()
    for b in range(ny):
        pltpu.make_async_copy(
            q_ref.at[:, pl.ds(pl.multiple_of((b * nx + x) * 2 * D, D), 2 * D)],
            qx.at[b, x],
            q_sent.at[1],
        ).start()

    for kv in range(2):
        ref = buf.at[slot(0, 0, kv, other)]
        pltpu.make_async_copy(ref, ref, part_sem.at[kv]).wait()
        for r in range(SPLIT):
            for d in range(2):
                send(buf.at[slot(0, 0, kv, other), pl.ds(r * rows, rows)], d, 1, kv, other, r)

    def ring_step(t):
        for turn in range(2):
            j = (c + turn) % 2
            for kv in range(2):
                for r in range(SPLIT):
                    for d in range(2):
                        arrived(d, t, kv, j, r)
                        send(buf.at[slot(d, t, kv, j), pl.ds(r * rows, rows)], d, t + 1, kv, j, r)

    def queries_along_y():
        blocks = qx.at[:, 0]
        for i in range(nx - 1):
            pltpu.make_async_copy(blocks, blocks, qx_sem.at[i]).wait()
        pltpu.make_async_copy(blocks, blocks, q_sent.at[1]).wait()
        for i, peer in enumerate(along_y):
            pltpu.make_async_remote_copy(
                src_ref=qx.at[(y + i + 1) % ny],
                dst_ref=qy.at[y],
                send_sem=q_sent.at[2],
                recv_sem=qy_sem.at[i],
                device_id=peer,
                device_id_type=MESH,
            ).start()
        pltpu.make_async_copy(qx.at[y], qy.at[y], q_sent.at[3]).start()

    def queries_to_partner():
        for i in range(ny - 1):
            pltpu.make_async_copy(qy.at[0], qy.at[0], qy_sem.at[i]).wait()
        pltpu.make_async_copy(qy.at[0], qy.at[0], q_sent.at[3]).wait()
        pltpu.make_async_remote_copy(
            src_ref=qy.at[:, :, :, cols(other)],
            dst_ref=qf.at[c],
            send_sem=q_sent.at[4],
            recv_sem=qf_sem,
            device_id=partner,
            device_id_type=MESH,
        ).start()
        pltpu.make_async_copy(qy.at[:, :, :, cols(c)], qf.at[c], q_sent.at[5]).start()

    def queries_ready():
        pltpu.make_async_copy(qf.at[0], qf.at[0], qf_sem).wait()
        pltpu.make_async_copy(qf.at[0], qf.at[0], q_sent.at[5]).wait()
        for j in range(2):
            block = qf[j].astype(jnp.float32).reshape(D, D)
            qt[:, j * D:(j + 1) * D] = block.T.astype(jnp.bfloat16)

    lane = lax.broadcasted_iota(jnp.int32, (1, 2 * D), 1)
    q_order = jnp.where(lane < D, order_ref[2 * z], order_ref[2 * z + 1])
    factor = math.log2(math.e) / math.sqrt(D)

    def scores(k):
        return jnp.dot(k, qt[...], preferred_element_type=jnp.float32)

    def mix(v, weight):
        return lax.dot_general(
            v, weight.astype(jnp.bfloat16), (((0,), (0,)), ((), ())),
            preferred_element_type=jnp.float32,
        )

    def diagonal():
        for kv in range(2):
            ref = buf.at[slot(0, 0, kv, c)]
            pltpu.make_async_copy(ref, ref, own_sem.at[1]).wait()
        k = buf[slot(0, 0, 0, 0):slot(0, 0, 0, 0) + 2].reshape(2 * D, D)
        v = buf[slot(0, 0, 1, 0):slot(0, 0, 1, 0) + 2].reshape(2 * D, D)
        key = lax.broadcasted_iota(jnp.int32, (2 * D, 2 * D), 0)
        query = lax.broadcasted_iota(jnp.int32, (2 * D, 2 * D), 1)
        key_pos = jnp.where(key < D, order_ref[2 * z] * D, order_ref[2 * z + 1] * D - D) + key
        query_pos = jnp.where(query < D, order_ref[2 * z] * D, order_ref[2 * z + 1] * D - D) + query
        s = jnp.where(key_pos <= query_pos, scores(k) * factor, NEG)
        top = jnp.max(s, axis=0, keepdims=True)
        weight = jnp.exp2(s - top)
        m_ref[...] = top
        l_ref[...] = jnp.sum(weight, axis=0, keepdims=True)
        acc_ref[...] = mix(v, weight)

    def attend(sources):
        old = m_ref[...]
        new = old
        parts = []
        for key_slot, value_slot, count, block in sources:
            s = scores(buf[pl.ds(key_slot, count)].reshape(count * D, D))
            for j in range(count):
                seen = order_ref[block + j] < q_order
                part = s[j * D:(j + 1) * D] * factor
                top = jnp.max(part, axis=0, keepdims=True)
                new = jnp.maximum(new, jnp.where(seen, top, NEG))
                parts.append((part, seen))
        total = jnp.zeros_like(new)
        mixed = None
        at = 0
        for key_slot, value_slot, count, block in sources:
            weights = []
            for j in range(count):
                part, seen = parts[at]
                at += 1
                weight = jnp.exp2(part - jnp.where(seen, new, -NEG))
                total = total + jnp.sum(weight, axis=0, keepdims=True)
                weights.append(weight)
            got = mix(buf[pl.ds(value_slot, count)].reshape(count * D, D), jnp.concatenate(weights, axis=0))
            mixed = got if mixed is None else mixed + got
        scale = jnp.exp2(old - new)
        m_ref[...] = new
        l_ref[...] = l_ref[...] * scale + total
        acc_ref[...] = acc_ref[...] * scale + mixed

    def attend_step(t):
        attend([
            (slot(0, t, 0, 0), slot(0, t, 1, 0), 2, 2 * ((z - t + nz) % nz)),
            (slot(1, t, 0, 0), slot(1, t, 1, 0), 2, 2 * ((z + t) % nz)),
        ])

    ring_step(1)
    queries_along_y()
    ring_step(2)
    queries_to_partner()
    ring_step(3)
    queries_ready()
    if COMPUTE:
        diagonal()

    def two_steps(t, _):
        ring_step(t)

        def one(u, _):
            if COMPUTE:
                attend_step(u)
            return 0

        lax.fori_loop(2 * t - 7, 2 * t - 5, one, 0)
        return 0

    lax.fori_loop(4, 6, two_steps, 0)

    def one_step(t, _):
        ring_step(t)
        if COMPUTE:
            attend_step(t - 1)
        return 0

    lax.fori_loop(6, half - 1, one_step, 0)

    for d in range(2):
        for kv in range(2):
            for r in range(SPLIT):
                arrived(d, half - 1, kv, d, r)
                send(buf.at[slot(d, half - 1, kv, d), pl.ds(r * rows, rows)], d, half, kv, d, r)
    if COMPUTE:
        attend_step(half - 2)
    for d in range(2):
        for kv in range(2):
            for r in range(SPLIT):
                arrived(d, half - 1, kv, 1 - d, r)
    if COMPUTE:
        attend_step(half - 1)
    for d in range(2):
        for kv in range(2):
            for r in range(SPLIT):
                arrived(d, half, kv, d, r)
    far = 2 * ((z + half) % nz)
    if COMPUTE:
        attend([
            (slot(0, half, 0, 0), slot(0, half, 1, 0), 1, far),
            (slot(1, half, 0, 1), slot(1, half, 1, 1), 1, far + 1),
        ])
    result = acc_ref[...] / l_ref[...]
    first = jnp.transpose(result[:, :D]).astype(jnp.bfloat16)
    second = jnp.transpose(result[:, D:]).astype(jnp.bfloat16)
    osend[...] = jnp.where(c == 0, second, first)
    give = pltpu.make_async_remote_copy(
        src_ref=osend,
        dst_ref=ost.at[:, cols(c)],
        send_sem=o_sem.at[0],
        recv_sem=o_sem.at[1],
        device_id=partner,
        device_id_type=MESH,
    )
    give.start()
    ost[:, cols(c)] = jnp.where(c == 0, first, second)

    count = 2 * (2 * half - 1)
    for d in range(2):
        ref = buf.at[pl.ds(0, count)]
        pltpu.make_async_copy(ref, ref, sent_sem.at[d]).wait()
    ref = buf.at[pl.ds(0, 2)]
    pltpu.make_async_copy(ref, ref, own_sem.at[0]).wait()
    ref = qx.at[pl.ds(0, nx - 1)]
    pltpu.make_async_copy(ref, ref, q_sent.at[0]).wait()
    ref = qy.at[pl.ds(0, ny - 1)]
    pltpu.make_async_copy(ref, ref, q_sent.at[2]).wait()
    pltpu.make_async_copy(qf.at[0], qf.at[0], q_sent.at[4]).wait()
    give.wait()
    done = pltpu.make_async_copy(ost, out_ref, o_sem.at[2])
    done.start()
    done.wait()


def body(nz, ny, nx, queries, keys, values, block_order):
    half = nz // 2
    blocks = 2 * (half + 1) * 2 * 2
    any_space = pl.BlockSpec(memory_space=pl.ANY)
    bf16, f32 = jnp.bfloat16, jnp.float32
    return pl.pallas_call(
        functools.partial(kernel, nz, ny, nx),
        out_shape=jax.ShapeDtypeStruct((D, 2 * D), bf16),
        in_specs=[pl.BlockSpec(memory_space=pltpu.SMEM), any_space, any_space, any_space],
        out_specs=any_space,
        scratch_shapes=[
            pltpu.VMEM((blocks, D, D), bf16),
            pltpu.VMEM((ny, nx, 8, 2 * D), bf16),
            pltpu.VMEM((ny, nx, 8, 2 * D), bf16),
            pltpu.VMEM((2, ny, nx, 8, D), bf16),
            pltpu.VMEM((D, 2 * D), bf16),
            pltpu.VMEM((1, 2 * D), f32),
            pltpu.VMEM((1, 2 * D), f32),
            pltpu.VMEM((D, 2 * D), f32),
            pltpu.VMEM((D, 2 * D), bf16),
            pltpu.VMEM((D, D), bf16),
            pltpu.SemaphoreType.DMA((blocks * SPLIT,)),
            pltpu.SemaphoreType.DMA((2,)),
            pltpu.SemaphoreType.DMA((2,)),
            pltpu.SemaphoreType.DMA((2,)),
            pltpu.SemaphoreType.DMA((nx - 1,)),
            pltpu.SemaphoreType.DMA((ny - 1,)),
            pltpu.SemaphoreType.DMA,
            pltpu.SemaphoreType.DMA((6,)),
            pltpu.SemaphoreType.DMA((3,)),
        ],
        compiler_params=pltpu.CompilerParams(
            collective_id=0, has_side_effects=True, vmem_limit_bytes=32 << 20
        ),
    )(block_order, queries, keys, values)


def solution(mesh):
    nz, ny, nx = mesh.shape["seq"] // 2, 4, mesh.shape["head"] // 4
    in_specs = (P(("seq", "head"), None), P("seq", "head"), P("seq", "head"), P())
    return jax.shard_map(
        functools.partial(body, nz, ny, nx),
        mesh=mesh, in_specs=in_specs, out_specs=P("seq", "head"), check_vma=False,
    )
```
